32 devices in a mesh: depth: 8 (over y, x, core), lane: 4 (over z).
Axes of the slice: x: 2, y: 2, z: 4, core: 2. Of those that a mesh axis runs over, the one named last changes fastest.
Arguments:
- fields_in: float32 [8, 4, 16, 1024], P('depth', None, 'lane'), may hold values from -6 to 6
- shot_data: float32 [4, 16, 2, 16, 1024], P(None, 'depth', None, 'lane'), may hold values from -1.5 to 1.5
- codes: int32 [4, 16, 16], P(None, None, 'lane'), may hold values from 0 to 15
- vel_index: int32 [32, 1024], P('depth'), may hold values from 0 to 63
- slowness_table: float32 [64], replicated, may hold values from 0.4 to 1
Outputs:
- fields_out: float32 [8, 4, 16, 1024], P('depth', None, 'lane')
- image: float32 [32, 1024], P(('depth', 'lane'))
The draws below stay inside these ranges and needn't reach their ends.
All inputs are finite; a program needn't handle non-finite values.
Results may differ from the reference program's by a relative error of at most 0.0003.
Values sent between devices are 32-bit elements; how exact they have to be, the bound alone decides.
A program may use at most 64 MiB of HBM per device.

```python
import math
import jax
import jax.numpy as jnp
from jax import lax

NX = 1024
STEPS = 4
TICKS = 4
LEVELS = 64
CODES = 16
SECTIONS = 8
NZ = 32
NF = 16
SHOTS = 16


def touch_ends(result, own_key, least, largest):
    longest = result.shape.index(max(result.shape))
    spots = []
    for shift in (0, 1):
        where = [jax.random.randint(jax.random.fold_in(own_key, axis), (), 0, length) for axis, length in enumerate(result.shape)]
        where[longest] = (where[longest] + shift) % result.shape[longest]
        spots.append(tuple(where))
    return result.at[spots[0]].set(least).at[spots[1]].set(largest)


def block_scale(stream_key, extent, split, smallest, largest):
    factor_of = 1.0
    for dim, shards_of in split:
        heights = jax.random.uniform(jax.random.fold_in(jax.random.fold_in(stream_key, 6), dim), (shards_of,), jnp.float32, smallest / len(split), largest / len(split))
        factor_of = factor_of * jnp.repeat(jnp.exp(heights), extent[dim] // shards_of).reshape((-1,) + (1,) * (len(extent) - 1 - dim))
    return factor_of


def scatter_about(key, shape, spread, limit, pieces=(), kind=jnp.bfloat16):
    result = jax.random.normal(key, shape, jnp.float32) * spread
    if len(pieces) > 0:
        result = block_scale(key, shape, pieces, -0.22, 0.18) * result
    return jnp.clip(result, min=-limit, max=limit).astype(kind)


def setup_inputs(seed: int = 0) -> dict:
    arg_keys = jax.random.split(jax.random.key(seed), 6)
    return {
        "fields_in": scatter_about(arg_keys[0], (SECTIONS, 4, NF, NX), 1.0, 6.0, ((0, 8), (2, 4)), jnp.float32),
        "shot_data": scatter_about(arg_keys[1], (TICKS, SHOTS, 2, NF, NX), SHOTS ** -0.5, 1.5, ((1, 8), (3, 4)), jnp.float32),
        "codes": touch_ends(jax.random.randint(arg_keys[2], (TICKS, SHOTS, NF), 0, CODES), jax.random.fold_in(arg_keys[2], 1), 0, CODES - 1).astype(jnp.int32),
        "vel_index": touch_ends(jax.random.randint(arg_keys[3], (NZ, NX), 0, LEVELS), jax.random.fold_in(arg_keys[3], 1), 0, LEVELS - 1).astype(jnp.int32),
        "slowness_table": jnp.clip(jnp.exp(jax.random.uniform(arg_keys[4], (LEVELS,), jnp.float32, math.log(0.4), math.log(1.0))), 0.4, 1.0),
    }


OMEGA_LO = 0.25
OMEGA_STEP = 0.07
DEPTH_STEP = 1.0
TWO_PI = 6.283185307179586

def wavenumbers(points):
    index = jnp.arange(points, dtype=jnp.int32)
    signed = jnp.where(index < points // 2, index, index - points)
    return signed.astype(jnp.float32) * (TWO_PI / points)

def reference(fields_in, shot_data, codes, vel_index, slowness_table):
    source = fields_in[:, 0] + 1j * fields_in[:, 1]
    receiver = fields_in[:, 2] + 1j * fields_in[:, 3]
    omegas = OMEGA_LO + OMEGA_STEP * jnp.arange(NF, dtype=jnp.int32).astype(jnp.float32)
    kx_sq = wavenumbers(NX) ** 2
    slowness = jnp.take(slowness_table, vel_index, axis=0).reshape(SECTIONS, STEPS, NX)
    angles = codes.astype(jnp.float32) * (TWO_PI / CODES)
    encode = jnp.cos(angles) + 1j * jnp.sin(angles)
    records = shot_data[:, :, 0] + 1j * shot_data[:, :, 1]
    rec_in = lax.optimization_barrier(jnp.sum(encode[:, :, :, None] * records, axis=1))
    spacing = NX // SHOTS
    marker = (jnp.arange(spacing, dtype=jnp.int32) == 0).astype(jnp.float32)
    src_in = (jnp.transpose(encode, (0, 2, 1))[:, :, :, None] * marker).reshape(TICKS, NF, NX)
    image = jnp.zeros((SECTIONS, STEPS, NX), jnp.float32)
    for tick_index in range(TICKS):
        for step_index in range(STEPS):
            slow_row = slowness[:, step_index]
            ref_slow = lax.optimization_barrier(jnp.mean(slow_row, axis=-1, keepdims=True))
            kz_sq = (omegas[None, :, None] * ref_slow[:, None, :]) ** 2 - kx_sq[None, None, :]
            phases = jnp.sqrt(jnp.maximum(kz_sq, 0.0)) * DEPTH_STEP
            damping = jnp.exp(-jnp.sqrt(jnp.maximum(-kz_sq, 0.0)) * DEPTH_STEP)
            lens_angle = omegas[None, :, None] * (slow_row - ref_slow)[:, None, :] * DEPTH_STEP
            turn = jnp.cos(phases) + 1j * jnp.sin(phases)
            lens_turn = jnp.cos(lens_angle) + 1j * jnp.sin(lens_angle)
            source = jnp.fft.ifft(jnp.fft.fft(source, axis=-1) * damping * turn, axis=-1) * lens_turn
            receiver = jnp.fft.ifft(jnp.fft.fft(receiver, axis=-1) * damping * jnp.conj(turn), axis=-1) * jnp.conj(lens_turn)
            contrib = lax.optimization_barrier(jnp.sum(jnp.real(source) * jnp.real(receiver) + jnp.imag(source) * jnp.imag(receiver), axis=1)) / NF
            image = image.at[:, step_index].add(contrib)
        source = jnp.concatenate([src_in[tick_index][None], source[:-1]], axis=0)
        receiver = jnp.concatenate([rec_in[tick_index][None], receiver[:-1]], axis=0)
    fields_out = jnp.stack([jnp.real(source), jnp.imag(source), jnp.real(receiver), jnp.imag(receiver)], axis=1)
    return (fields_out, image.reshape(NZ, NX))
```

```python
import functools
import math

import jax
import jax.numpy as jnp
import numpy as np
from jax import lax
from jax.experimental import pallas as pl
from jax.experimental.pallas import tpu as pltpu
from jax.sharding import PartitionSpec as P

MESH = pl.DeviceIdType.MESH
CODES = 16
OMEGA_LO = 0.25
OMEGA_STEP = 0.07
DEPTH_STEP = 1.0
TWO_PI = 6.283185307179586
LANES = 128
BF16 = jnp.bfloat16
F32 = jnp.float32


def dft_matrix(count):
    turns = np.outer(np.arange(count), np.arange(count)) % count
    angle = turns * (2.0 * np.pi / count)
    c, s = np.cos(angle), np.sin(angle)
    full = np.block([[c, -s], [s, c]]).astype(np.float32)
    high = full.astype(BF16)
    low = (full - high.astype(np.float32)).astype(BF16)
    return high, low


def twist_tables(outer, inner):
    angle = np.outer(np.arange(outer), np.arange(inner)) * (2.0 * np.pi / (outer * inner))
    return np.stack([np.cos(angle), np.sin(angle)]).astype(np.float32)


def sincos(x):
    n = jnp.floor(x * (2.0 / math.pi) + 0.5)
    r = x - n * 1.5703125
    r = r - n * 4.837512969970703e-4
    r = r - n * 7.549789948768648e-8
    z = r * r
    s = r + r * z * (-1.6666654611e-1 + z * (8.3321608736e-3 + z * -1.9515295891e-4))
    c = 1.0 - 0.5 * z + z * z * (
        4.166664568298827e-2 + z * (-1.388731625493765e-3 + z * 2.443315711809948e-5)
    )
    q = n - 4.0 * jnp.floor(n * 0.25)
    odd = (q == 1.0) | (q == 3.0)
    sin_base = jnp.where(odd, c, s)
    cos_base = jnp.where(odd, s, c)
    sin_out = jnp.where(q >= 2.0, -sin_base, sin_base)
    cos_out = jnp.where((q == 1.0) | (q == 2.0), -cos_base, cos_base)
    return sin_out, cos_out


def dft_across(re, im):
    count = len(re)
    if count == 1:
        return re, im
    even_re, even_im = dft_across(re[0::2], im[0::2])
    odd_re, odd_im = dft_across(re[1::2], im[1::2])
    half = count // 2
    out_re, out_im = [None] * count, [None] * count
    for k in range(half):
        c = math.cos(2.0 * math.pi * k / count)
        s = math.sin(2.0 * math.pi * k / count)
        a, b = odd_re[k], odd_im[k]
        if k == 0:
            tr, ti = a, b
        elif 4 * k == count:
            tr, ti = b, -a
        elif 8 * k == count:
            tr, ti = (a + b) * c, (b - a) * c
        elif 8 * k == 3 * count:
            tr, ti = (b - a) * s, -(a + b) * s
        else:
            tr, ti = a * c + b * s, b * c - a * s
        out_re[k], out_im[k] = even_re[k] + tr, even_im[k] + ti
        out_re[k + half], out_im[k + half] = even_re[k] - tr, even_im[k] - ti
    return out_re, out_im


def kernel(
    sizes,
    codes_ref, table_ref,
    fields_ref, shots_ref, vel_ref, src_ref, whi_ref, wlo_ref, twist_ref,
    out_ref, image_ref,
    prop, lens, sends, recvs, enc, rec_out, rec_in, image_acc, image_send, image_in,
    send_sem, recv_sem, rec_send_sem, rec_sem, image_send_sem, image_sem,
):
    depth_n, lane_n, freqs, ticks, steps, shots_here, levels, points = sizes
    outer = points // LANES
    half_outer = outer // 2
    per_lane = steps // lane_n
    depth = lax.axis_index("depth")
    lane = lax.axis_index("lane")
    freq_total = freqs * lane_n
    rows = 2 * freqs

    barrier = pltpu.get_barrier_semaphore()

    def greet(d, l):
        pl.semaphore_signal(barrier, inc=1, device_id=(d, l), device_id_type=MESH)

    @pl.when(depth == 0)
    def _():
        for d in range(1, depth_n):
            greet(d, lane)

    @pl.when(depth > 0)
    def _():
        greet(0, lane)

    @pl.when(depth > 1)
    def _():
        greet(depth - 1, lane)

    @pl.when((depth > 0) & (depth < depth_n - 1))
    def _():
        greet(depth + 1, lane)

    for off in range(1, lane_n):
        greet(depth, lax.rem(lane + off, lane_n))

    row = lax.broadcasted_iota(jnp.int32, (rows, LANES), 0)
    freq_row = jnp.where(row >= freqs, row - freqs, row)
    for t in range(ticks):
        for j in range(shots_here):
            code = jnp.zeros((rows, LANES), jnp.int32)
            for f in range(freqs):
                value = codes_ref[t, depth * shots_here + j, f]
                code = jnp.where(freq_row == f, value, code)
            sin_e, cos_e = sincos(code.astype(F32) * (TWO_PI / CODES))
            enc[t, j, 0] = cos_e
            enc[t, j, 1] = sin_e

    def chunk(a):
        return slice(a * LANES, (a + 1) * LANES)

    for t in range(ticks):
        for a in range(half_outer):
            total_re, total_im = None, None
            for j in range(shots_here):
                pair = [
                    jnp.concatenate(
                        [shots_ref[t, j, c, :, chunk(a)], shots_ref[t, j, c, :, chunk(a + half_outer)]],
                        axis=0,
                    )
                    for c in range(2)
                ]
                c, s = enc[t, j, 0], enc[t, j, 1]
                re = c * pair[0] - s * pair[1]
                im = c * pair[1] + s * pair[0]
                total_re = re if total_re is None else total_re + re
                total_im = im if total_im is None else total_im + im
            rec_out[t, 0, a] = total_re
            rec_out[t, 1, a] = -total_im

    greeted = jnp.where(
        depth == 0,
        depth_n - 1,
        1 + (depth > 1).astype(jnp.int32) + (depth < depth_n - 1).astype(jnp.int32),
    ) + (lane_n - 1)
    pl.semaphore_wait(barrier, greeted)

    def rec_copy(t):
        return pltpu.make_async_remote_copy(
            src_ref=rec_out.at[t],
            dst_ref=rec_in.at[t, jnp.maximum(depth - 1, 0)],
            send_sem=rec_send_sem.at[t],
            recv_sem=rec_sem.at[t],
            device_id=(0, lane),
            device_id_type=MESH,
        )

    @pl.when(depth > 0)
    def _():
        for t in range(ticks):
            rec_copy(t).start()

    omega = OMEGA_LO + OMEGA_STEP * (lane * freqs + freq_row).astype(F32)
    index = vel_ref[...]
    slow_all = jnp.zeros((steps, points), F32)
    for l in range(levels):
        slow_all = jnp.where(index == l, table_ref[l], slow_all)
    ref_all = jnp.sum(slow_all, axis=1, keepdims=True) * (1.0 / points)
    column = lax.broadcasted_iota(jnp.int32, (rows, LANES), 1)
    for z in range(steps):
        ref_z = ref_all[z : z + 1, :]
        omega_ref = omega * ref_z
        for a in range(outer):
            m = a + outer * column
            m = jnp.where(m < points // 2, m, m - points)
            kx = m.astype(F32) * (TWO_PI / points)
            kz_sq = omega_ref * omega_ref - kx * kx
            phase = jnp.sqrt(jnp.maximum(kz_sq, 0.0)) * DEPTH_STEP
            damp = jnp.exp(-jnp.sqrt(jnp.maximum(-kz_sq, 0.0)) * DEPTH_STEP) * (1.0 / points)
            s, c = sincos(phase)
            prop[z, 0, a] = damp * c
            prop[z, 1, a] = damp * s
            angle = omega * (slow_all[z : z + 1, chunk(a)] - ref_z) * DEPTH_STEP
            s, c = sincos(angle)
            lens[z, 0, a] = c
            lens[z, 1, a] = s

    image_acc[...] = jnp.zeros_like(image_acc)

    def inner_dft(re, im):
        left = jnp.concatenate(re, axis=0)
        right = jnp.concatenate(im, axis=0)
        x = jnp.concatenate([left, right], axis=1)
        high = x.astype(BF16)
        low = (x - high.astype(F32)).astype(BF16)
        y = jnp.dot(high, whi_ref[...], preferred_element_type=F32)
        y = y + jnp.dot(low, whi_ref[...], preferred_element_type=F32)
        y = y + jnp.dot(high, wlo_ref[...], preferred_element_type=F32)
        y_re = [y[a * rows : (a + 1) * rows, :LANES] for a in range(outer)]
        y_im = [y[a * rows : (a + 1) * rows, LANES:] for a in range(outer)]
        return y_re, y_im

    def times(re, im, c, s):
        return re * c - im * s, re * s + im * c

    def step(k, state):
        re, im = list(state[:outer]), list(state[outer:])
        re, im = dft_across(re, im)
        for a in range(1, outer):
            c, s = twist_ref[0, a : a + 1, :], twist_ref[1, a : a + 1, :]
            re[a], im[a] = times(re[a], im[a], c, -s)
        re, im = inner_dft(re, im)
        for a in range(outer):
            re[a], im[a] = times(re[a], im[a], prop[k, 0, a], prop[k, 1, a])
        im, re = inner_dft(im, re)
        for a in range(1, outer):
            c, s = twist_ref[0, a : a + 1, :], twist_ref[1, a : a + 1, :]
            re[a], im[a] = times(re[a], im[a], c, s)
        im, re = dft_across(im, re)
        for a in range(outer):
            re[a], im[a] = times(re[a], im[a], lens[k, 0, a], lens[k, 1, a])
            image_acc[k, a] += re[a] * pltpu.roll(re[a], freqs, 0) - im[a] * pltpu.roll(
                im[a], freqs, 0
            )
        return tuple(re) + tuple(im)

    def field_copy(t):
        return pltpu.make_async_remote_copy(
            src_ref=sends.at[t],
            dst_ref=recvs.at[t],
            send_sem=send_sem.at[t],
            recv_sem=recv_sem.at[t],
            device_id=(jnp.minimum(depth + 1, depth_n - 1), lane),
            device_id_type=MESH,
        )

    def image_copy(k):
        return pltpu.make_async_remote_copy(
            src_ref=image_send.at[k],
            dst_ref=image_in.at[k % per_lane, lane],
            send_sem=image_send_sem.at[k],
            recv_sem=image_sem.at[k % per_lane, lane],
            device_id=(depth, k // per_lane),
            device_id_type=MESH,
        )

    for t in range(ticks):
        if t == 0:
            re = [
                jnp.concatenate([fields_ref[0, 0, :, chunk(a)], fields_ref[0, 2, :, chunk(a)]], axis=0)
                for a in range(outer)
            ]
            im = [
                jnp.concatenate([fields_ref[0, 1, :, chunk(a)], -fields_ref[0, 3, :, chunk(a)]], axis=0)
                for a in range(outer)
            ]
        else:
            re = [recvs[t - 1, 0, a] for a in range(outer)]
            im = [recvs[t - 1, 1, a] for a in range(outer)]
        state = lax.fori_loop(0, steps, step, tuple(re) + tuple(im))
        for a in range(outer):
            sends[t, 0, a] = state[a]
            sends[t, 1, a] = state[outer + a]

        @pl.when(depth < depth_n - 1)
        def _():
            field_copy(t).start()

        if t == ticks - 1:
            for k in range(steps):
                packed = jnp.zeros((outer, LANES), F32)
                place = lax.broadcasted_iota(jnp.int32, (outer, LANES), 0)
                for a in range(outer):
                    total = jnp.sum(image_acc[k, a][:freqs], axis=0, keepdims=True)
                    packed = jnp.where(place == a, total, packed)
                image_send[k] = packed * (1.0 / freq_total)

                @pl.when(lane != k // per_lane)
                def _():
                    image_copy(k).start()

        @pl.when(depth == 0)
        def _():
            pltpu.make_async_copy(rec_in.at[t], rec_in.at[t], rec_sem.at[t]).wait()
            for c in range(2):
                for a in range(half_outer):
                    total = rec_out[t, c, a]
                    for d in range(depth_n - 1):
                        total = total + rec_in[t, d, c, a]
                    for side in range(2):
                        where = a + side * half_outer
                        rec = total[side * freqs : (side + 1) * freqs]
                        recvs[t, c, where] = jnp.concatenate(
                            [src_ref[t, c, :, chunk(where)], rec], axis=0
                        )

        @pl.when(depth > 0)
        def _():
            pltpu.make_async_copy(recvs.at[t], recvs.at[t], recv_sem.at[t]).wait()

    for a in range(outer):
        re, im = recvs[ticks - 1, 0, a], recvs[ticks - 1, 1, a]
        out_ref[0, 0, :, chunk(a)] = re[:freqs]
        out_ref[0, 1, :, chunk(a)] = im[:freqs]
        out_ref[0, 2, :, chunk(a)] = re[freqs:]
        out_ref[0, 3, :, chunk(a)] = -im[freqs:]

    for i in range(per_lane):
        total = image_send[lane * per_lane + i]
        for l in range(lane_n):

            @pl.when(lane != l)
            def _():
                pltpu.make_async_copy(
                    image_in.at[i, l], image_in.at[i, l], image_sem.at[i, l]
                ).wait()

            total = total + jnp.where(lane != l, image_in[i, l], 0.0)
        for a in range(outer):
            image_ref[i : i + 1, chunk(a)] = total[a : a + 1, :]

    for t in range(ticks):

        @pl.when(depth < depth_n - 1)
        def _():
            field_copy(t).wait_send()

        @pl.when(depth > 0)
        def _():
            rec_copy(t).wait_send()

    for k in range(steps):

        @pl.when(lane != k // per_lane)
        def _():
            image_copy(k).wait_send()


def solution(mesh):
    depth_n, lane_n = mesh.shape["depth"], mesh.shape["lane"]

    def per_device(fields_in, shot_data, codes, vel_index, slowness_table):
        _, planes, freqs, points = fields_in.shape
        ticks, shots_here = shot_data.shape[0], shot_data.shape[1]
        shot_total = codes.shape[1]
        steps = vel_index.shape[0]
        levels = slowness_table.shape[0]
        outer = points // LANES
        rows = 2 * freqs
        per_lane = steps // lane_n
        angles = jnp.transpose(codes, (0, 2, 1)).astype(F32) * (TWO_PI / CODES)
        marker = (jnp.arange(points // shot_total) == 0).astype(F32)
        src = jnp.stack([jnp.cos(angles), jnp.sin(angles)], axis=1)
        src = (src[..., None] * marker).reshape(ticks, 2, freqs, points)
        high, low = dft_matrix(LANES)
        twist = twist_tables(outer, LANES)
        sizes = (depth_n, lane_n, freqs, ticks, steps, shots_here, levels, points)
        vmem = pl.BlockSpec(memory_space=pltpu.VMEM)
        smem = pl.BlockSpec(memory_space=pltpu.SMEM)
        return pl.pallas_call(
            functools.partial(kernel, sizes),
            out_shape=(
                jax.ShapeDtypeStruct(fields_in.shape, F32),
                jax.ShapeDtypeStruct((per_lane, points), F32),
            ),
            in_specs=[smem, smem] + [vmem] * 7,
            out_specs=(vmem, vmem),
            scratch_shapes=[
                pltpu.VMEM((steps, 2, outer, rows, LANES), F32),
                pltpu.VMEM((steps, 2, outer, rows, LANES), F32),
                pltpu.VMEM((ticks, 2, outer, rows, LANES), F32),
                pltpu.VMEM((ticks, 2, outer, rows, LANES), F32),
                pltpu.VMEM((ticks, shots_here, 2, rows, LANES), F32),
                pltpu.VMEM((ticks, 2, outer // 2, rows, LANES), F32),
                pltpu.VMEM((ticks, depth_n - 1, 2, outer // 2, rows, LANES), F32),
                pltpu.VMEM((steps, outer, rows, LANES), F32),
                pltpu.VMEM((steps, outer, LANES), F32),
                pltpu.VMEM((per_lane, lane_n, outer, LANES), F32),
                pltpu.SemaphoreType.DMA((ticks,)),
                pltpu.SemaphoreType.DMA((ticks,)),
                pltpu.SemaphoreType.DMA((ticks,)),
                pltpu.SemaphoreType.DMA((ticks,)),
                pltpu.SemaphoreType.DMA((steps,)),
                pltpu.SemaphoreType.DMA((per_lane, lane_n)),
            ],
            compiler_params=pltpu.CompilerParams(collective_id=0, has_side_effects=True),
            name="migrate",
        )(
            codes, slowness_table, fields_in, shot_data, vel_index, src,
            jnp.asarray(high), jnp.asarray(low), jnp.asarray(twist),
        )

    return jax.shard_map(
        per_device,
        mesh=mesh,
        in_specs=(
            P("depth", None, "lane", None),
            P(None, "depth", None, "lane", None),
            P(None, None, "lane"),
            P("depth", None),
            P(),
        ),
        out_specs=(P("depth", None, "lane", None), P(("depth", "lane"), None)),
        check_vma=False,
    )
```

```python
import functools
import math

import jax
import jax.numpy as jnp
import numpy as np
from jax import lax
from jax.experimental import pallas as pl
from jax.experimental.pallas import tpu as pltpu
from jax.sharding import PartitionSpec as P

MESH = pl.DeviceIdType.MESH
CODES = 16
OMEGA_LO = 0.25
OMEGA_STEP = 0.07
DEPTH_STEP = 1.0
TWO_PI = 6.283185307179586
LANES = 128
BF16 = jnp.bfloat16
F32 = jnp.float32


def dft_matrix(count):
    turns = np.outer(np.arange(count), np.arange(count)) % count
    angle = turns * (2.0 * np.pi / count)
    c, s = np.cos(angle), np.sin(angle)
    full = np.block([[c, -s], [s, c]]).astype(np.float32)
    high = full.astype(BF16)
    low = (full - high.astype(np.float32)).astype(BF16)
    return high, low


def twist_tables(outer, inner):
    angle = np.outer(np.arange(outer), np.arange(inner)) * (2.0 * np.pi / (outer * inner))
    return np.stack([np.cos(angle), np.sin(angle)]).astype(np.float32)


def sincos(x):
    n = jnp.floor(x * (2.0 / math.pi) + 0.5)
    r = x - n * 1.5703125
    r = r - n * 4.837512969970703e-4
    r = r - n * 7.549789948768648e-8
    z = r * r
    s = r + r * z * (-1.6666654611e-1 + z * (8.3321608736e-3 + z * -1.9515295891e-4))
    c = 1.0 - 0.5 * z + z * z * (
        4.166664568298827e-2 + z * (-1.388731625493765e-3 + z * 2.443315711809948e-5)
    )
    q = n - 4.0 * jnp.floor(n * 0.25)
    odd = (q == 1.0) | (q == 3.0)
    sin_base = jnp.where(odd, c, s)
    cos_base = jnp.where(odd, s, c)
    sin_out = jnp.where(q >= 2.0, -sin_base, sin_base)
    cos_out = jnp.where((q == 1.0) | (q == 2.0), -cos_base, cos_base)
    return sin_out, cos_out


def dft_across(re, im):
    count = len(re)
    if count == 1:
        return re, im
    even_re, even_im = dft_across(re[0::2], im[0::2])
    odd_re, odd_im = dft_across(re[1::2], im[1::2])
    half = count // 2
    out_re, out_im = [None] * count, [None] * count
    for k in range(half):
        c = math.cos(2.0 * math.pi * k / count)
        s = math.sin(2.0 * math.pi * k / count)
        a, b = odd_re[k], odd_im[k]
        if k == 0:
            tr, ti = a, b
        elif 4 * k == count:
            tr, ti = b, -a
        elif 8 * k == count:
            tr, ti = (a + b) * c, (b - a) * c
        elif 8 * k == 3 * count:
            tr, ti = (b - a) * s, -(a + b) * s
        else:
            tr, ti = a * c + b * s, b * c - a * s
        out_re[k], out_im[k] = even_re[k] + tr, even_im[k] + ti
        out_re[k + half], out_im[k + half] = even_re[k] - tr, even_im[k] - ti
    return out_re, out_im


def kernel(
    sizes,
    codes_hbm, table_hbm, shots_hbm, vel_hbm, fields_hbm, whi_hbm, wlo_hbm, twist_hbm,
    out_ref, image_ref,
    codes_ref, code_rows, table_ref, shots_ref, vel_ref, fields_ref, whi_ref, wlo_ref, twist_ref,
    load_sem,
    prop, lens, sends, recvs, rec_out, rec_in, image_acc, image_send, image_in,
    send_sem, recv_sem, rec_send_sem, rec_sem, image_send_sem, image_sem,
):
    depth_n, lane_n, freqs, ticks, steps, shots_here, levels, points = sizes
    outer = points // LANES
    half_outer = outer // 2
    per_lane = steps // lane_n
    depth = lax.axis_index("depth")
    lane = lax.axis_index("lane")
    freq_total = freqs * lane_n
    rows = 2 * freqs

    loads = [
        pltpu.make_async_copy(src, dst, load_sem.at[i])
        for i, (src, dst) in enumerate(
            (
                (codes_hbm, codes_ref),
                (shots_hbm, shots_ref),
                (table_hbm, table_ref),
                (vel_hbm, vel_ref),
                (fields_hbm, fields_ref),
                (whi_hbm, whi_ref),
                (wlo_hbm, wlo_ref),
                (twist_hbm, twist_ref),
                (codes_hbm, code_rows),
            )
        )
    ]
    for load in loads:
        load.start()

    barrier = pltpu.get_barrier_semaphore()

    def greet(d, l):
        pl.semaphore_signal(barrier, inc=1, device_id=(d, l), device_id_type=MESH)

    @pl.when(depth == 0)
    def _():
        for d in range(1, depth_n):
            greet(d, lane)

    @pl.when(depth > 0)
    def _():
        greet(0, lane)

    @pl.when(depth > 1)
    def _():
        greet(depth - 1, lane)

    @pl.when((depth > 0) & (depth < depth_n - 1))
    def _():
        greet(depth + 1, lane)

    for off in range(1, lane_n):
        greet(depth, lax.rem(lane + off, lane_n))

    row = lax.broadcasted_iota(jnp.int32, (rows, LANES), 0)
    freq_row = jnp.where(row >= freqs, row - freqs, row)

    def chunk(a):
        return slice(a * LANES, (a + 1) * LANES)

    def encode(t):
        waves = []
        for j in range(shots_here):
            code = jnp.zeros((rows, LANES), jnp.int32)
            for f in range(freqs):
                value = codes_ref[t, f, depth * shots_here + j]
                code = jnp.where(freq_row == f, value, code)
            waves.append(sincos(code.astype(F32) * (TWO_PI / CODES)))
        for a in range(half_outer):
            total_re, total_im = None, None
            for j in range(shots_here):
                pair = [
                    jnp.concatenate(
                        [shots_ref[t, j, c, :, chunk(a)], shots_ref[t, j, c, :, chunk(a + half_outer)]],
                        axis=0,
                    )
                    for c in range(2)
                ]
                s, c = waves[j]
                re = c * pair[0] - s * pair[1]
                im = c * pair[1] + s * pair[0]
                total_re = re if total_re is None else total_re + re
                total_im = im if total_im is None else total_im + im
            rec_out[t, 0, a] = total_re
            rec_out[t, 1, a] = -total_im

    def rec_copy(t):
        return pltpu.make_async_remote_copy(
            src_ref=rec_out.at[t],
            dst_ref=rec_in.at[t, jnp.maximum(depth - 1, 0)],
            send_sem=rec_send_sem.at[t],
            recv_sem=rec_sem.at[t],
            device_id=(0, lane),
            device_id_type=MESH,
        )

    loads[0].wait()
    loads[1].wait()
    encode(0)
    greeted = jnp.where(
        depth == 0,
        depth_n - 1,
        1 + (depth > 1).astype(jnp.int32) + (depth < depth_n - 1).astype(jnp.int32),
    ) + (lane_n - 1)
    pl.semaphore_wait(barrier, greeted)

    @pl.when(depth > 0)
    def _():
        rec_copy(0).start()

    for t in range(1, ticks):
        encode(t)
    for load in loads[2:]:
        load.wait()

    omega = OMEGA_LO + OMEGA_STEP * (lane * freqs + freq_row).astype(F32)
    index = vel_ref[...]
    slow_all = jnp.zeros((steps, points), F32)
    for l in range(levels):
        slow_all = jnp.where(index == l, table_ref[l], slow_all)
    ref_all = jnp.sum(slow_all, axis=1, keepdims=True) * (1.0 / points)
    column = lax.broadcasted_iota(jnp.int32, (rows, LANES), 1)
    for z in range(steps):
        ref_z = ref_all[z : z + 1, :]
        omega_ref = omega * ref_z
        for a in range(outer):
            m = a + outer * column
            m = jnp.where(m < points // 2, m, m - points)
            kx = m.astype(F32) * (TWO_PI / points)
            kz_sq = omega_ref * omega_ref - kx * kx
            phase = jnp.sqrt(jnp.maximum(kz_sq, 0.0)) * DEPTH_STEP
            damp = jnp.exp(-jnp.sqrt(jnp.maximum(-kz_sq, 0.0)) * DEPTH_STEP) * (1.0 / points)
            s, c = sincos(phase)
            prop[z, 0, a] = damp * c
            prop[z, 1, a] = damp * s
            angle = omega * (slow_all[z : z + 1, chunk(a)] - ref_z) * DEPTH_STEP
            s, c = sincos(angle)
            lens[z, 0, a] = c
            lens[z, 1, a] = s

    image_acc[...] = jnp.zeros_like(image_acc)

    def inner_dft(re, im):
        left = jnp.concatenate(re, axis=0)
        right = jnp.concatenate(im, axis=0)
        x = jnp.concatenate([left, right], axis=1)
        high = x.astype(BF16)
        low = (x - high.astype(F32)).astype(BF16)
        both = jnp.dot(
            jnp.concatenate([high, low], axis=0), whi_ref[...], preferred_element_type=F32
        )
        y = both[: outer * rows] + both[outer * rows :]
        y = y + jnp.dot(high, wlo_ref[...], preferred_element_type=F32)
        y_re = [y[a * rows : (a + 1) * rows, :LANES] for a in range(outer)]
        y_im = [y[a * rows : (a + 1) * rows, LANES:] for a in range(outer)]
        return y_re, y_im

    def times(re, im, c, s):
        return re * c - im * s, re * s + im * c

    def step(k, state):
        re, im = list(state[:outer]), list(state[outer:])
        re, im = dft_across(re, im)
        for a in range(1, outer):
            c, s = twist_ref[0, a : a + 1, :], twist_ref[1, a : a + 1, :]
            re[a], im[a] = times(re[a], im[a], c, -s)
        re, im = inner_dft(re, im)
        for a in range(outer):
            re[a], im[a] = times(re[a], im[a], prop[k, 0, a], prop[k, 1, a])
        im, re = inner_dft(im, re)
        for a in range(1, outer):
            c, s = twist_ref[0, a : a + 1, :], twist_ref[1, a : a + 1, :]
            re[a], im[a] = times(re[a], im[a], c, s)
        im, re = dft_across(im, re)
        for a in range(outer):
            re[a], im[a] = times(re[a], im[a], lens[k, 0, a], lens[k, 1, a])
            image_acc[k, a] += re[a] * pltpu.roll(re[a], freqs, 0) - im[a] * pltpu.roll(
                im[a], freqs, 0
            )
        return tuple(re) + tuple(im)

    def field_copy(t):
        return pltpu.make_async_remote_copy(
            src_ref=sends.at[t],
            dst_ref=recvs.at[t],
            send_sem=send_sem.at[t],
            recv_sem=recv_sem.at[t],
            device_id=(jnp.minimum(depth + 1, depth_n - 1), lane),
            device_id_type=MESH,
        )

    def image_copy(k):
        return pltpu.make_async_remote_copy(
            src_ref=image_send.at[k],
            dst_ref=image_in.at[k % per_lane, lane],
            send_sem=image_send_sem.at[k],
            recv_sem=image_sem.at[k % per_lane, lane],
            device_id=(depth, k // per_lane),
            device_id_type=MESH,
        )

    def sources():
        shot_total = code_rows.shape[2]
        spacing = points // shot_total
        lane_index = lax.broadcasted_iota(jnp.int32, (freqs, LANES), 1)
        for t in range(ticks):
            sin_e, cos_e = sincos(code_rows[t].astype(F32) * (TWO_PI / CODES))
            for c, wave in enumerate((cos_e, sin_e)):
                for a in range(outer):
                    value = jnp.zeros((freqs, LANES), F32)
                    for j in range(shot_total):
                        place = j * spacing - a * LANES
                        if 0 <= place < LANES:
                            value = jnp.where(lane_index == place, wave[:, j : j + 1], value)
                    recvs[t, c, a, :freqs] = value

    for t in range(ticks):
        if t == 0:
            re = [
                jnp.concatenate([fields_ref[0, 0, :, chunk(a)], fields_ref[0, 2, :, chunk(a)]], axis=0)
                for a in range(outer)
            ]
            im = [
                jnp.concatenate([fields_ref[0, 1, :, chunk(a)], -fields_ref[0, 3, :, chunk(a)]], axis=0)
                for a in range(outer)
            ]
        else:
            re = [recvs[t - 1, 0, a] for a in range(outer)]
            im = [recvs[t - 1, 1, a] for a in range(outer)]
        state = lax.fori_loop(0, steps, step, tuple(re) + tuple(im))
        for a in range(outer):
            sends[t, 0, a] = state[a]
            sends[t, 1, a] = state[outer + a]

        @pl.when(depth < depth_n - 1)
        def _():
            field_copy(t).start()

        if t + 1 < ticks:

            @pl.when(depth > 0)
            def _():
                rec_copy(t + 1).start()

        if t == ticks - 1:
            for k in range(steps):
                packed = jnp.zeros((outer, LANES), F32)
                place = lax.broadcasted_iota(jnp.int32, (outer, LANES), 0)
                for a in range(outer):
                    total = jnp.sum(image_acc[k, a][:freqs], axis=0, keepdims=True)
                    packed = jnp.where(place == a, total, packed)
                image_send[k] = packed * (1.0 / freq_total)

                @pl.when(lane != k // per_lane)
                def _():
                    image_copy(k).start()

        @pl.when(depth == 0)
        def _():
            if t == 0:
                sources()
            pltpu.make_async_copy(rec_in.at[t], rec_in.at[t], rec_sem.at[t]).wait()
            for c in range(2):
                for a in range(half_outer):
                    total = rec_out[t, c, a]
                    for d in range(depth_n - 1):
                        total = total + rec_in[t, d, c, a]
                    for side in range(2):
                        where = a + side * half_outer
                        rec = total[side * freqs : (side + 1) * freqs]
                        recvs[t, c, where, freqs:] = rec

        @pl.when(depth > 0)
        def _():
            pltpu.make_async_copy(recvs.at[t], recvs.at[t], recv_sem.at[t]).wait()

    for a in range(outer):
        re, im = recvs[ticks - 1, 0, a], recvs[ticks - 1, 1, a]
        out_ref[0, 0, :, chunk(a)] = re[:freqs]
        out_ref[0, 1, :, chunk(a)] = im[:freqs]
        out_ref[0, 2, :, chunk(a)] = re[freqs:]
        out_ref[0, 3, :, chunk(a)] = -im[freqs:]

    for i in range(per_lane):
        total = image_send[lane * per_lane + i]
        for l in range(lane_n):

            @pl.when(lane != l)
            def _():
                pltpu.make_async_copy(
                    image_in.at[i, l], image_in.at[i, l], image_sem.at[i, l]
                ).wait()

            total = total + jnp.where(lane != l, image_in[i, l], 0.0)
        for a in range(outer):
            image_ref[i : i + 1, chunk(a)] = total[a : a + 1, :]

    for t in range(ticks):

        @pl.when(depth < depth_n - 1)
        def _():
            field_copy(t).wait_send()

        @pl.when(depth > 0)
        def _():
            rec_copy(t).wait_send()

    for k in range(steps):

        @pl.when(lane != k // per_lane)
        def _():
            image_copy(k).wait_send()


def solution(mesh):
    depth_n, lane_n = mesh.shape["depth"], mesh.shape["lane"]

    def per_device(fields_in, shot_data, codes, vel_index, slowness_table):
        _, planes, freqs, points = fields_in.shape
        ticks, shots_here = shot_data.shape[0], shot_data.shape[1]
        shot_total = codes.shape[1]
        steps = vel_index.shape[0]
        levels = slowness_table.shape[0]
        outer = points // LANES
        rows = 2 * freqs
        per_lane = steps // lane_n
        codes = jnp.transpose(codes, (0, 2, 1))
        high, low = dft_matrix(LANES)
        twist = twist_tables(outer, LANES)
        sizes = (depth_n, lane_n, freqs, ticks, steps, shots_here, levels, points)
        anywhere = pl.BlockSpec(memory_space=pl.ANY)
        vmem = pl.BlockSpec(memory_space=pltpu.VMEM)
        fields_out, image = pl.pallas_call(
            functools.partial(kernel, sizes),
            out_shape=(
                pltpu.VMEM(fields_in.shape, F32),
                pltpu.VMEM((per_lane, points), F32),
            ),
            in_specs=[anywhere] * 8,
            out_specs=(vmem, vmem),
            scratch_shapes=[
                pltpu.SMEM(codes.shape, jnp.int32),
                pltpu.VMEM(codes.shape, jnp.int32),
                pltpu.SMEM(slowness_table.shape, F32),
                pltpu.VMEM(shot_data.shape, F32),
                pltpu.VMEM(vel_index.shape, jnp.int32),
                pltpu.VMEM(fields_in.shape, F32),
                pltpu.VMEM(high.shape, BF16),
                pltpu.VMEM(low.shape, BF16),
                pltpu.VMEM(twist.shape, F32),
                pltpu.SemaphoreType.DMA((9,)),
                pltpu.VMEM((steps, 2, outer, rows, LANES), F32),
                pltpu.VMEM((steps, 2, outer, rows, LANES), F32),
                pltpu.VMEM((ticks, 2, outer, rows, LANES), F32),
                pltpu.VMEM((ticks, 2, outer, rows, LANES), F32),
                pltpu.VMEM((ticks, 2, outer // 2, rows, LANES), F32),
                pltpu.VMEM((ticks, depth_n - 1, 2, outer // 2, rows, LANES), F32),
                pltpu.VMEM((steps, outer, rows, LANES), F32),
                pltpu.VMEM((steps, outer, LANES), F32),
                pltpu.VMEM((per_lane, lane_n, outer, LANES), F32),
                pltpu.SemaphoreType.DMA((ticks,)),
                pltpu.SemaphoreType.DMA((ticks,)),
                pltpu.SemaphoreType.DMA((ticks,)),
                pltpu.SemaphoreType.DMA((ticks,)),
                pltpu.SemaphoreType.DMA((steps,)),
                pltpu.SemaphoreType.DMA((per_lane, lane_n)),
            ],
            compiler_params=pltpu.CompilerParams(collective_id=0, has_side_effects=True),
            name="migrate",
        )(
            codes, slowness_table, shot_data, vel_index, fields_in,
            jnp.asarray(high), jnp.asarray(low), jnp.asarray(twist),
        )
        return fields_out, image

    return jax.shard_map(
        per_device,
        mesh=mesh,
        in_specs=(
            P("depth", None, "lane", None),
            P(None, "depth", None, "lane", None),
            P(None, None, "lane"),
            P("depth", None),
            P(),
        ),
        out_specs=(P("depth", None, "lane", None), P(("depth", "lane"), None)),
        check_vma=False,
    )
```

```python
import functools
import math

import jax
import jax.numpy as jnp
import numpy as np
from jax import lax
from jax.experimental import pallas as pl
from jax.experimental.pallas import tpu as pltpu
from jax.sharding import PartitionSpec as P

MESH = pl.DeviceIdType.MESH
CODES = 16
OMEGA_LO = 0.25
OMEGA_STEP = 0.07
DEPTH_STEP = 1.0
TWO_PI = 6.283185307179586
LANES = 128
BF16 = jnp.bfloat16
F32 = jnp.float32


def dft_matrix(count):
    turns = np.outer(np.arange(count), np.arange(count)) % count
    angle = turns * (2.0 * np.pi / count)
    c, s = np.cos(angle), np.sin(angle)
    full = np.block([[c, -s], [s, c]]).astype(np.float32)
    high = full.astype(BF16)
    low = (full - high.astype(np.float32)).astype(BF16)
    return high, low


def twist_tables(outer, inner):
    angle = np.outer(np.arange(outer), np.arange(inner)) * (2.0 * np.pi / (outer * inner))
    return np.stack([np.cos(angle), np.sin(angle)]).astype(np.float32)


def sincos(x):
    n = jnp.floor(x * (2.0 / math.pi) + 0.5)
    r = x - n * 1.5703125
    r = r - n * 4.837512969970703e-4
    r = r - n * 7.549789948768648e-8
    z = r * r
    s = r + r * z * (-1.6666654611e-1 + z * (8.3321608736e-3 + z * -1.9515295891e-4))
    c = 1.0 - 0.5 * z + z * z * (
        4.166664568298827e-2 + z * (-1.388731625493765e-3 + z * 2.443315711809948e-5)
    )
    q = n - 4.0 * jnp.floor(n * 0.25)
    odd = (q == 1.0) | (q == 3.0)
    sin_base = jnp.where(odd, c, s)
    cos_base = jnp.where(odd, s, c)
    sin_out = jnp.where(q >= 2.0, -sin_base, sin_base)
    cos_out = jnp.where((q == 1.0) | (q == 2.0), -cos_base, cos_base)
    return sin_out, cos_out


def dft_across(re, im):
    count = len(re)
    if count == 1:
        return re, im
    even_re, even_im = dft_across(re[0::2], im[0::2])
    odd_re, odd_im = dft_across(re[1::2], im[1::2])
    half = count // 2
    out_re, out_im = [None] * count, [None] * count
    for k in range(half):
        c = math.cos(2.0 * math.pi * k / count)
        s = math.sin(2.0 * math.pi * k / count)
        a, b = odd_re[k], odd_im[k]
        if k == 0:
            tr, ti = a, b
        elif 4 * k == count:
            tr, ti = b, -a
        elif 8 * k == count:
            tr, ti = (a + b) * c, (b - a) * c
        elif 8 * k == 3 * count:
            tr, ti = (b - a) * s, -(a + b) * s
        else:
            tr, ti = a * c + b * s, b * c - a * s
        out_re[k], out_im[k] = even_re[k] + tr, even_im[k] + ti
        out_re[k + half], out_im[k + half] = even_re[k] - tr, even_im[k] - ti
    return out_re, out_im


def kernel(
    sizes,
    codes_hbm, table_hbm, shots_hbm, vel_hbm, fields_hbm, whi_hbm, wlo_hbm, twist_hbm,
    out_ref, image_ref,
    codes_ref, code_rows, table_ref, shots_ref, vel_ref, fields_ref, whi_ref, wlo_ref, twist_ref,
    load_sem,
    prop, lens, sends, recvs, rec_out, rec_in, image_acc, image_send, image_in,
    send_sem, recv_sem, rec_send_sem, rec_sem, image_send_sem, image_sem,
):
    depth_n, lane_n, freqs, ticks, steps, shots_here, levels, points = sizes
    outer = points // LANES
    half_outer = outer // 2
    per_lane = steps // lane_n
    depth = lax.axis_index("depth")
    lane = lax.axis_index("lane")
    freq_total = freqs * lane_n
    rows = 2 * freqs

    loads = [
        pltpu.make_async_copy(src, dst, load_sem.at[i])
        for i, (src, dst) in enumerate(
            (
                (codes_hbm, codes_ref),
                (shots_hbm, shots_ref),
                (table_hbm, table_ref),
                (vel_hbm, vel_ref),
                (fields_hbm, fields_ref),
                (whi_hbm, whi_ref),
                (wlo_hbm, wlo_ref),
                (twist_hbm, twist_ref),
                (codes_hbm, code_rows),
            )
        )
    ]
    for load in loads:
        load.start()

    barrier = pltpu.get_barrier_semaphore()

    def greet(d, l):
        pl.semaphore_signal(barrier, inc=1, device_id=(d, l), device_id_type=MESH)

    @pl.when(depth == 0)
    def _():
        for d in range(1, depth_n):
            greet(d, lane)

    @pl.when(depth > 0)
    def _():
        greet(0, lane)

    @pl.when(depth > 1)
    def _():
        greet(depth - 1, lane)

    @pl.when((depth > 0) & (depth < depth_n - 1))
    def _():
        greet(depth + 1, lane)

    for off in range(1, lane_n):
        greet(depth, lax.rem(lane + off, lane_n))

    row = lax.broadcasted_iota(jnp.int32, (rows, LANES), 0)
    freq_row = jnp.where(row >= freqs, row - freqs, row)

    def chunk(a):
        return slice(a * LANES, (a + 1) * LANES)

    def encode(t):
        waves = []
        for j in range(shots_here):
            code = jnp.zeros((rows, LANES), jnp.int32)
            for f in range(freqs):
                value = codes_ref[t, f, depth * shots_here + j]
                code = jnp.where(freq_row == f, value, code)
            waves.append(sincos(code.astype(F32) * (TWO_PI / CODES)))
        for a in range(half_outer):
            total_re, total_im = None, None
            for j in range(shots_here):
                pair = [
                    jnp.concatenate(
                        [shots_ref[t, j, c, :, chunk(a)], shots_ref[t, j, c, :, chunk(a + half_outer)]],
                        axis=0,
                    )
                    for c in range(2)
                ]
                s, c = waves[j]
                re = c * pair[0] - s * pair[1]
                im = c * pair[1] + s * pair[0]
                total_re = re if total_re is None else total_re + re
                total_im = im if total_im is None else total_im + im
            rec_out[t, 0, a] = total_re
            rec_out[t, 1, a] = -total_im

    def rec_copy(t):
        return pltpu.make_async_remote_copy(
            src_ref=rec_out.at[t],
            dst_ref=rec_in.at[t, jnp.maximum(depth - 1, 0)],
            send_sem=rec_send_sem.at[t],
            recv_sem=rec_sem.at[t],
            device_id=(0, lane),
            device_id_type=MESH,
        )

    loads[0].wait()
    loads[1].wait()
    encode(0)
    for t in range(1, ticks):
        encode(t)
    for load in loads[2:]:
        load.wait()

    omega = OMEGA_LO + OMEGA_STEP * (lane * freqs + freq_row).astype(F32)
    index = vel_ref[...]
    slow_all = jnp.zeros((steps, points), F32)
    for l in range(levels):
        slow_all = jnp.where(index == l, table_ref[l], slow_all)
    ref_all = jnp.sum(slow_all, axis=1, keepdims=True) * (1.0 / points)
    column = lax.broadcasted_iota(jnp.int32, (rows, LANES), 1)
    for z in range(steps):
        ref_z = ref_all[z : z + 1, :]
        omega_ref = omega * ref_z
        for a in range(outer):
            m = a + outer * column
            m = jnp.where(m < points // 2, m, m - points)
            kx = m.astype(F32) * (TWO_PI / points)
            kz_sq = omega_ref * omega_ref - kx * kx
            phase = jnp.sqrt(jnp.maximum(kz_sq, 0.0)) * DEPTH_STEP
            damp = jnp.exp(-jnp.sqrt(jnp.maximum(-kz_sq, 0.0)) * DEPTH_STEP) * (1.0 / points)
            s, c = sincos(phase)
            prop[z, 0, a] = damp * c
            prop[z, 1, a] = damp * s
            angle = omega * (slow_all[z : z + 1, chunk(a)] - ref_z) * DEPTH_STEP
            s, c = sincos(angle)
            lens[z, 0, a] = c
            lens[z, 1, a] = s

    image_acc[...] = jnp.zeros_like(image_acc)

    def inner_dft(re, im):
        left = jnp.concatenate(re, axis=0)
        right = jnp.concatenate(im, axis=0)
        x = jnp.concatenate([left, right], axis=1)
        high = x.astype(BF16)
        low = (x - high.astype(F32)).astype(BF16)
        both = jnp.dot(
            jnp.concatenate([high, low], axis=0), whi_ref[...], preferred_element_type=F32
        )
        y = both[: outer * rows] + both[outer * rows :]
        y = y + jnp.dot(high, wlo_ref[...], preferred_element_type=F32)
        y_re = [y[a * rows : (a + 1) * rows, :LANES] for a in range(outer)]
        y_im = [y[a * rows : (a + 1) * rows, LANES:] for a in range(outer)]
        return y_re, y_im

    def times(re, im, c, s):
        return re * c - im * s, re * s + im * c

    def step(k, state):
        re, im = list(state[:outer]), list(state[outer:])
        re, im = dft_across(re, im)
        for a in range(1, outer):
            c, s = twist_ref[0, a : a + 1, :], twist_ref[1, a : a + 1, :]
            re[a], im[a] = times(re[a], im[a], c, -s)
        re, im = inner_dft(re, im)
        for a in range(outer):
            re[a], im[a] = times(re[a], im[a], prop[k, 0, a], prop[k, 1, a])
        im, re = inner_dft(im, re)
        for a in range(1, outer):
            c, s = twist_ref[0, a : a + 1, :], twist_ref[1, a : a + 1, :]
            re[a], im[a] = times(re[a], im[a], c, s)
        im, re = dft_across(im, re)
        for a in range(outer):
            re[a], im[a] = times(re[a], im[a], lens[k, 0, a], lens[k, 1, a])
            image_acc[k, a] += re[a] * pltpu.roll(re[a], freqs, 0) - im[a] * pltpu.roll(
                im[a], freqs, 0
            )
        return tuple(re) + tuple(im)

    def field_copy(t):
        return pltpu.make_async_remote_copy(
            src_ref=sends.at[t],
            dst_ref=recvs.at[t],
            send_sem=send_sem.at[t],
            recv_sem=recv_sem.at[t],
            device_id=(jnp.minimum(depth + 1, depth_n - 1), lane),
            device_id_type=MESH,
        )

    def image_copy(k):
        return pltpu.make_async_remote_copy(
            src_ref=image_send.at[k],
            dst_ref=image_in.at[k % per_lane, lane],
            send_sem=image_send_sem.at[k],
            recv_sem=image_sem.at[k % per_lane, lane],
            device_id=(depth, k // per_lane),
            device_id_type=MESH,
        )

    def sources():
        shot_total = code_rows.shape[2]
        spacing = points // shot_total
        lane_index = lax.broadcasted_iota(jnp.int32, (freqs, LANES), 1)
        for t in range(ticks):
            sin_e, cos_e = sincos(code_rows[t].astype(F32) * (TWO_PI / CODES))
            for c, wave in enumerate((cos_e, sin_e)):
                for a in range(outer):
                    value = jnp.zeros((freqs, LANES), F32)
                    for j in range(shot_total):
                        place = j * spacing - a * LANES
                        if 0 <= place < LANES:
                            value = jnp.where(lane_index == place, wave[:, j : j + 1], value)
                    recvs[t, c, a, :freqs] = value

    for t in range(ticks):
        if t == 0:
            re = [
                jnp.concatenate([fields_ref[0, 0, :, chunk(a)], fields_ref[0, 2, :, chunk(a)]], axis=0)
                for a in range(outer)
            ]
            im = [
                jnp.concatenate([fields_ref[0, 1, :, chunk(a)], -fields_ref[0, 3, :, chunk(a)]], axis=0)
                for a in range(outer)
            ]
        else:
            re = [recvs[t - 1, 0, a] for a in range(outer)]
            im = [recvs[t - 1, 1, a] for a in range(outer)]
        state = lax.fori_loop(0, steps, step, tuple(re) + tuple(im))
        for a in range(outer):
            sends[t, 0, a] = state[a]
            sends[t, 1, a] = state[outer + a]

        if t == 0:
            greeted = jnp.where(
                depth == 0,
                depth_n - 1,
                1 + (depth > 1).astype(jnp.int32) + (depth < depth_n - 1).astype(jnp.int32),
            ) + (lane_n - 1)
            pl.semaphore_wait(barrier, greeted)

            @pl.when(depth > 0)
            def _():
                rec_copy(0).start()

        @pl.when(depth < depth_n - 1)
        def _():
            field_copy(t).start()

        if t + 1 < ticks:

            @pl.when(depth > 0)
            def _():
                rec_copy(t + 1).start()

        if t == ticks - 1:
            for k in range(steps):
                packed = jnp.zeros((outer, LANES), F32)
                place = lax.broadcasted_iota(jnp.int32, (outer, LANES), 0)
                for a in range(outer):
                    total = jnp.sum(image_acc[k, a][:freqs], axis=0, keepdims=True)
                    packed = jnp.where(place == a, total, packed)
                image_send[k] = packed * (1.0 / freq_total)

                @pl.when(lane != k // per_lane)
                def _():
                    image_copy(k).start()

        @pl.when(depth == 0)
        def _():
            if t == 0:
                sources()
            pltpu.make_async_copy(rec_in.at[t], rec_in.at[t], rec_sem.at[t]).wait()
            for c in range(2):
                for a in range(half_outer):
                    total = rec_out[t, c, a]
                    for d in range(depth_n - 1):
                        total = total + rec_in[t, d, c, a]
                    for side in range(2):
                        where = a + side * half_outer
                        rec = total[side * freqs : (side + 1) * freqs]
                        recvs[t, c, where, freqs:] = rec

        @pl.when(depth > 0)
        def _():
            pltpu.make_async_copy(recvs.at[t], recvs.at[t], recv_sem.at[t]).wait()

    for a in range(outer):
        re, im = recvs[ticks - 1, 0, a], recvs[ticks - 1, 1, a]
        out_ref[0, 0, :, chunk(a)] = re[:freqs]
        out_ref[0, 1, :, chunk(a)] = im[:freqs]
        out_ref[0, 2, :, chunk(a)] = re[freqs:]
        out_ref[0, 3, :, chunk(a)] = -im[freqs:]

    for i in range(per_lane):
        total = image_send[lane * per_lane + i]
        for l in range(lane_n):

            @pl.when(lane != l)
            def _():
                pltpu.make_async_copy(
                    image_in.at[i, l], image_in.at[i, l], image_sem.at[i, l]
                ).wait()

            total = total + jnp.where(lane != l, image_in[i, l], 0.0)
        for a in range(outer):
            image_ref[i : i + 1, chunk(a)] = total[a : a + 1, :]

    for t in range(ticks):

        @pl.when(depth < depth_n - 1)
        def _():
            field_copy(t).wait_send()

        @pl.when(depth > 0)
        def _():
            rec_copy(t).wait_send()

    for k in range(steps):

        @pl.when(lane != k // per_lane)
        def _():
            image_copy(k).wait_send()


def solution(mesh):
    depth_n, lane_n = mesh.shape["depth"], mesh.shape["lane"]

    def per_device(fields_in, shot_data, codes, vel_index, slowness_table):
        _, planes, freqs, points = fields_in.shape
        ticks, shots_here = shot_data.shape[0], shot_data.shape[1]
        shot_total = codes.shape[1]
        steps = vel_index.shape[0]
        levels = slowness_table.shape[0]
        outer = points // LANES
        rows = 2 * freqs
        per_lane = steps // lane_n
        codes = jnp.transpose(codes, (0, 2, 1))
        high, low = dft_matrix(LANES)
        twist = twist_tables(outer, LANES)
        sizes = (depth_n, lane_n, freqs, ticks, steps, shots_here, levels, points)
        anywhere = pl.BlockSpec(memory_space=pl.ANY)
        vmem = pl.BlockSpec(memory_space=pltpu.VMEM)
        fields_out, image = pl.pallas_call(
            functools.partial(kernel, sizes),
            out_shape=(
                pltpu.VMEM(fields_in.shape, F32),
                pltpu.VMEM((per_lane, points), F32),
            ),
            in_specs=[anywhere] * 8,
            out_specs=(vmem, vmem),
            scratch_shapes=[
                pltpu.SMEM(codes.shape, jnp.int32),
                pltpu.VMEM(codes.shape, jnp.int32),
                pltpu.SMEM(slowness_table.shape, F32),
                pltpu.VMEM(shot_data.shape, F32),
                pltpu.VMEM(vel_index.shape, jnp.int32),
                pltpu.VMEM(fields_in.shape, F32),
                pltpu.VMEM(high.shape, BF16),
                pltpu.VMEM(low.shape, BF16),
                pltpu.VMEM(twist.shape, F32),
                pltpu.SemaphoreType.DMA((9,)),
                pltpu.VMEM((steps, 2, outer, rows, LANES), F32),
                pltpu.VMEM((steps, 2, outer, rows, LANES), F32),
                pltpu.VMEM((ticks, 2, outer, rows, LANES), F32),
                pltpu.VMEM((ticks, 2, outer, rows, LANES), F32),
                pltpu.VMEM((ticks, 2, outer // 2, rows, LANES), F32),
                pltpu.VMEM((ticks, depth_n - 1, 2, outer // 2, rows, LANES), F32),
                pltpu.VMEM((steps, outer, rows, LANES), F32),
                pltpu.VMEM((steps, outer, LANES), F32),
                pltpu.VMEM((per_lane, lane_n, outer, LANES), F32),
                pltpu.SemaphoreType.DMA((ticks,)),
                pltpu.SemaphoreType.DMA((ticks,)),
                pltpu.SemaphoreType.DMA((ticks,)),
                pltpu.SemaphoreType.DMA((ticks,)),
                pltpu.SemaphoreType.DMA((steps,)),
                pltpu.SemaphoreType.DMA((per_lane, lane_n)),
            ],
            compiler_params=pltpu.CompilerParams(collective_id=0, has_side_effects=True),
            name="migrate",
        )(
            codes, slowness_table, shot_data, vel_index, fields_in,
            jnp.asarray(high), jnp.asarray(low), jnp.asarray(twist),
        )
        return fields_out, image

    return jax.shard_map(
        per_device,
        mesh=mesh,
        in_specs=(
            P("depth", None, "lane", None),
            P(None, "depth", None, "lane", None),
            P(None, None, "lane"),
            P("depth", None),
            P(),
        ),
        out_specs=(P("depth", None, "lane", None), P(("depth", "lane"), None)),
        check_vma=False,
    )
```

```python
import functools
import math

import jax
import jax.numpy as jnp
import numpy as np
from jax import lax
from jax.experimental import pallas as pl
from jax.experimental.pallas import tpu as pltpu
from jax.sharding import PartitionSpec as P

MESH = pl.DeviceIdType.MESH
CODES = 16
OMEGA_LO = 0.25
OMEGA_STEP = 0.07
DEPTH_STEP = 1.0
TWO_PI = 6.283185307179586
LANES = 128
BF16 = jnp.bfloat16
F32 = jnp.float32


def dft_matrix(count):
    turns = np.outer(np.arange(count), np.arange(count)) % count
    angle = turns * (2.0 * np.pi / count)
    c, s = np.cos(angle), np.sin(angle)
    full = np.block([[c, -s], [s, c]]).astype(np.float32)
    high = full.astype(BF16)
    low = (full - high.astype(np.float32)).astype(BF16)
    return high, low


def twist_tables(outer, inner):
    angle = np.outer(np.arange(outer), np.arange(inner)) * (2.0 * np.pi / (outer * inner))
    return np.stack([np.cos(angle), np.sin(angle)]).astype(np.float32)


def sincos(x):
    n = jnp.floor(x * (2.0 / math.pi) + 0.5)
    r = x - n * 1.5703125
    r = r - n * 4.837512969970703e-4
    r = r - n * 7.549789948768648e-8
    z = r * r
    s = r + r * z * (-1.6666654611e-1 + z * (8.3321608736e-3 + z * -1.9515295891e-4))
    c = 1.0 - 0.5 * z + z * z * (
        4.166664568298827e-2 + z * (-1.388731625493765e-3 + z * 2.443315711809948e-5)
    )
    q = n - 4.0 * jnp.floor(n * 0.25)
    odd = (q == 1.0) | (q == 3.0)
    sin_base = jnp.where(odd, c, s)
    cos_base = jnp.where(odd, s, c)
    sin_out = jnp.where(q >= 2.0, -sin_base, sin_base)
    cos_out = jnp.where((q == 1.0) | (q == 2.0), -cos_base, cos_base)
    return sin_out, cos_out


def dft_across(re, im):
    count = len(re)
    if count == 1:
        return re, im
    even_re, even_im = dft_across(re[0::2], im[0::2])
    odd_re, odd_im = dft_across(re[1::2], im[1::2])
    half = count // 2
    out_re, out_im = [None] * count, [None] * count
    for k in range(half):
        c = math.cos(2.0 * math.pi * k / count)
        s = math.sin(2.0 * math.pi * k / count)
        a, b = odd_re[k], odd_im[k]
        if k == 0:
            tr, ti = a, b
        elif 4 * k == count:
            tr, ti = b, -a
        elif 8 * k == count:
            tr, ti = (a + b) * c, (b - a) * c
        elif 8 * k == 3 * count:
            tr, ti = (b - a) * s, -(a + b) * s
        else:
            tr, ti = a * c + b * s, b * c - a * s
        out_re[k], out_im[k] = even_re[k] + tr, even_im[k] + ti
        out_re[k + half], out_im[k + half] = even_re[k] - tr, even_im[k] - ti
    return out_re, out_im


def kernel(
    sizes,
    codes_hbm, table_hbm, shots_hbm, vel_hbm, fields_hbm, whi_hbm, wlo_hbm, twist_hbm,
    out_ref, image_ref,
    codes_ref, code_rows, table_ref, shots_ref, vel_ref, fields_ref, whi_ref, wlo_ref, twist_ref,
    load_sem,
    prop, lens, sends, recvs, rec_out, rec_in, image_acc, image_send, image_in,
    send_sem, recv_sem, rec_send_sem, rec_sem, image_send_sem, image_sem,
):
    depth_n, lane_n, freqs, ticks, steps, shots_here, levels, points = sizes
    outer = points // LANES
    half_outer = outer // 2
    per_lane = steps // lane_n
    depth = lax.axis_index("depth")
    lane = lax.axis_index("lane")
    freq_total = freqs * lane_n
    rows = 2 * freqs

    loads = [
        pltpu.make_async_copy(src, dst, load_sem.at[i])
        for i, (src, dst) in enumerate(
            (
                (codes_hbm, codes_ref),
                (shots_hbm, shots_ref),
                (table_hbm, table_ref),
                (vel_hbm, vel_ref),
                (fields_hbm, fields_ref),
                (whi_hbm, whi_ref),
                (wlo_hbm, wlo_ref),
                (twist_hbm, twist_ref),
                (codes_hbm, code_rows),
            )
        )
    ]
    for load in loads:
        load.start()

    barrier = pltpu.get_barrier_semaphore()

    def greet(d, l):
        pl.semaphore_signal(barrier, inc=1, device_id=(d, l), device_id_type=MESH)

    @pl.when(depth == 0)
    def _():
        for d in range(1, depth_n):
            greet(d, lane)

    @pl.when(depth > 0)
    def _():
        greet(0, lane)

    @pl.when(depth > 1)
    def _():
        greet(depth - 1, lane)

    @pl.when((depth > 0) & (depth < depth_n - 1))
    def _():
        greet(depth + 1, lane)

    for off in range(1, lane_n):
        greet(depth, lax.rem(lane + off, lane_n))

    row = lax.broadcasted_iota(jnp.int32, (rows, LANES), 0)
    freq_row = jnp.where(row >= freqs, row - freqs, row)

    def chunk(a):
        return slice(a * LANES, (a + 1) * LANES)

    def encode(t):
        waves = []
        for j in range(shots_here):
            code = jnp.zeros((rows, LANES), jnp.int32)
            for f in range(freqs):
                value = codes_ref[t, f, depth * shots_here + j]
                code = jnp.where(freq_row == f, value, code)
            waves.append(sincos(code.astype(F32) * (TWO_PI / CODES)))
        for a in range(half_outer):
            total_re, total_im = None, None
            for j in range(shots_here):
                pair = [
                    jnp.concatenate(
                        [shots_ref[t, j, c, :, chunk(a)], shots_ref[t, j, c, :, chunk(a + half_outer)]],
                        axis=0,
                    )
                    for c in range(2)
                ]
                s, c = waves[j]
                re = c * pair[0] - s * pair[1]
                im = c * pair[1] + s * pair[0]
                total_re = re if total_re is None else total_re + re
                total_im = im if total_im is None else total_im + im
            rec_out[t, 0, a] = total_re
            rec_out[t, 1, a] = -total_im

    def rec_copy(t):
        return pltpu.make_async_remote_copy(
            src_ref=rec_out.at[t],
            dst_ref=rec_in.at[t, jnp.maximum(depth - 1, 0)],
            send_sem=rec_send_sem.at[t],
            recv_sem=rec_sem.at[t],
            device_id=(0, lane),
            device_id_type=MESH,
        )

    loads[0].wait()
    loads[1].wait()
    encode(0)
    greeted = jnp.where(
        depth == 0,
        depth_n - 1,
        1 + (depth > 1).astype(jnp.int32) + (depth < depth_n - 1).astype(jnp.int32),
    ) + (lane_n - 1)
    pl.semaphore_wait(barrier, greeted)

    @pl.when(depth > 0)
    def _():
        rec_copy(0).start()

    for load in loads[2:]:
        load.wait()

    omega = OMEGA_LO + OMEGA_STEP * (lane * freqs + freq_row).astype(F32)
    index = vel_ref[...]
    slow_all = jnp.zeros((steps, points), F32)
    for l in range(levels):
        slow_all = jnp.where(index == l, table_ref[l], slow_all)
    ref_all = jnp.sum(slow_all, axis=1, keepdims=True) * (1.0 / points)
    column = lax.broadcasted_iota(jnp.int32, (rows, LANES), 1)
    for z in range(steps):
        ref_z = ref_all[z : z + 1, :]
        omega_ref = omega * ref_z
        for a in range(outer):
            m = a + outer * column
            m = jnp.where(m < points // 2, m, m - points)
            kx = m.astype(F32) * (TWO_PI / points)
            kz_sq = omega_ref * omega_ref - kx * kx
            phase = jnp.sqrt(jnp.maximum(kz_sq, 0.0)) * DEPTH_STEP
            damp = jnp.exp(-jnp.sqrt(jnp.maximum(-kz_sq, 0.0)) * DEPTH_STEP) * (1.0 / points)
            s, c = sincos(phase)
            prop[z, 0, a] = damp * c
            prop[z, 1, a] = damp * s
            angle = omega * (slow_all[z : z + 1, chunk(a)] - ref_z) * DEPTH_STEP
            s, c = sincos(angle)
            lens[z, 0, a] = c
            lens[z, 1, a] = s

    image_acc[...] = jnp.zeros_like(image_acc)

    def inner_dft(re, im):
        left = jnp.concatenate(re, axis=0)
        right = jnp.concatenate(im, axis=0)
        x = jnp.concatenate([left, right], axis=1)
        high = x.astype(BF16)
        low = (x - high.astype(F32)).astype(BF16)
        both = jnp.dot(
            jnp.concatenate([high, low], axis=0), whi_ref[...], preferred_element_type=F32
        )
        y = both[: outer * rows] + both[outer * rows :]
        y = y + jnp.dot(high, wlo_ref[...], preferred_element_type=F32)
        y_re = [y[a * rows : (a + 1) * rows, :LANES] for a in range(outer)]
        y_im = [y[a * rows : (a + 1) * rows, LANES:] for a in range(outer)]
        return y_re, y_im

    def times(re, im, c, s):
        return re * c - im * s, re * s + im * c

    def step(k, state):
        re, im = list(state[:outer]), list(state[outer:])
        re, im = dft_across(re, im)
        for a in range(1, outer):
            c, s = twist_ref[0, a : a + 1, :], twist_ref[1, a : a + 1, :]
            re[a], im[a] = times(re[a], im[a], c, -s)
        re, im = inner_dft(re, im)
        for a in range(outer):
            re[a], im[a] = times(re[a], im[a], prop[k, 0, a], prop[k, 1, a])
        im, re = inner_dft(im, re)
        for a in range(1, outer):
            c, s = twist_ref[0, a : a + 1, :], twist_ref[1, a : a + 1, :]
            re[a], im[a] = times(re[a], im[a], c, s)
        im, re = dft_across(im, re)
        for a in range(outer):
            re[a], im[a] = times(re[a], im[a], lens[k, 0, a], lens[k, 1, a])
            image_acc[k, a] += re[a] * pltpu.roll(re[a], freqs, 0) - im[a] * pltpu.roll(
                im[a], freqs, 0
            )
        return tuple(re) + tuple(im)

    def field_copy(t):
        return pltpu.make_async_remote_copy(
            src_ref=sends.at[t],
            dst_ref=recvs.at[t],
            send_sem=send_sem.at[t],
            recv_sem=recv_sem.at[t],
            device_id=(jnp.minimum(depth + 1, depth_n - 1), lane),
            device_id_type=MESH,
        )

    def image_copy(k):
        return pltpu.make_async_remote_copy(
            src_ref=image_send.at[k],
            dst_ref=image_in.at[k % per_lane, lane],
            send_sem=image_send_sem.at[k],
            recv_sem=image_sem.at[k % per_lane, lane],
            device_id=(depth, k // per_lane),
            device_id_type=MESH,
        )

    def sources():
        shot_total = code_rows.shape[2]
        spacing = points // shot_total
        lane_index = lax.broadcasted_iota(jnp.int32, (freqs, LANES), 1)
        for t in range(ticks):
            sin_e, cos_e = sincos(code_rows[t].astype(F32) * (TWO_PI / CODES))
            for c, wave in enumerate((cos_e, sin_e)):
                for a in range(outer):
                    value = jnp.zeros((freqs, LANES), F32)
                    for j in range(shot_total):
                        place = j * spacing - a * LANES
                        if 0 <= place < LANES:
                            value = jnp.where(lane_index == place, wave[:, j : j + 1], value)
                    recvs[t, c, a, :freqs] = value

    for t in range(ticks):
        if t == 0:
            re = [
                jnp.concatenate([fields_ref[0, 0, :, chunk(a)], fields_ref[0, 2, :, chunk(a)]], axis=0)
                for a in range(outer)
            ]
            im = [
                jnp.concatenate([fields_ref[0, 1, :, chunk(a)], -fields_ref[0, 3, :, chunk(a)]], axis=0)
                for a in range(outer)
            ]
        else:
            re = [recvs[t - 1, 0, a] for a in range(outer)]
            im = [recvs[t - 1, 1, a] for a in range(outer)]
        state = lax.fori_loop(0, steps, step, tuple(re) + tuple(im))
        for a in range(outer):
            sends[t, 0, a] = state[a]
            sends[t, 1, a] = state[outer + a]

        @pl.when(depth < depth_n - 1)
        def _():
            field_copy(t).start()

        if t + 1 < ticks:
            encode(t + 1)

        if t == ticks - 1:
            for k in range(steps):
                packed = jnp.zeros((outer, LANES), F32)
                place = lax.broadcasted_iota(jnp.int32, (outer, LANES), 0)
                for a in range(outer):
                    total = jnp.sum(image_acc[k, a][:freqs], axis=0, keepdims=True)
                    packed = jnp.where(place == a, total, packed)
                image_send[k] = packed * (1.0 / freq_total)

                @pl.when(lane != k // per_lane)
                def _():
                    image_copy(k).start()

        @pl.when(depth == 0)
        def _():
            if t == 0:
                sources()
            pltpu.make_async_copy(rec_in.at[t], rec_in.at[t], rec_sem.at[t]).wait()
            for c in range(2):
                for a in range(half_outer):
                    total = rec_out[t, c, a]
                    for d in range(depth_n - 1):
                        total = total + rec_in[t, d, c, a]
                    for side in range(2):
                        where = a + side * half_outer
                        rec = total[side * freqs : (side + 1) * freqs]
                        recvs[t, c, where, freqs:] = rec

        @pl.when(depth > 0)
        def _():
            pltpu.make_async_copy(recvs.at[t], recvs.at[t], recv_sem.at[t]).wait()
            if t + 1 < ticks:
                rec_copy(t + 1).start()

    for a in range(outer):
        re, im = recvs[ticks - 1, 0, a], recvs[ticks - 1, 1, a]
        out_ref[0, 0, :, chunk(a)] = re[:freqs]
        out_ref[0, 1, :, chunk(a)] = im[:freqs]
        out_ref[0, 2, :, chunk(a)] = re[freqs:]
        out_ref[0, 3, :, chunk(a)] = -im[freqs:]

    for i in range(per_lane):
        total = image_send[lane * per_lane + i]
        for l in range(lane_n):

            @pl.when(lane != l)
            def _():
                pltpu.make_async_copy(
                    image_in.at[i, l], image_in.at[i, l], image_sem.at[i, l]
                ).wait()

            total = total + jnp.where(lane != l, image_in[i, l], 0.0)
        for a in range(outer):
            image_ref[i : i + 1, chunk(a)] = total[a : a + 1, :]

    for t in range(ticks):

        @pl.when(depth < depth_n - 1)
        def _():
            field_copy(t).wait_send()

        @pl.when(depth > 0)
        def _():
            rec_copy(t).wait_send()

    for k in range(steps):

        @pl.when(lane != k // per_lane)
        def _():
            image_copy(k).wait_send()


def solution(mesh):
    depth_n, lane_n = mesh.shape["depth"], mesh.shape["lane"]

    def per_device(fields_in, shot_data, codes, vel_index, slowness_table):
        _, planes, freqs, points = fields_in.shape
        ticks, shots_here = shot_data.shape[0], shot_data.shape[1]
        shot_total = codes.shape[1]
        steps = vel_index.shape[0]
        levels = slowness_table.shape[0]
        outer = points // LANES
        rows = 2 * freqs
        per_lane = steps // lane_n
        codes = jnp.transpose(codes, (0, 2, 1))
        high, low = dft_matrix(LANES)
        twist = twist_tables(outer, LANES)
        sizes = (depth_n, lane_n, freqs, ticks, steps, shots_here, levels, points)
        anywhere = pl.BlockSpec(memory_space=pl.ANY)
        vmem = pl.BlockSpec(memory_space=pltpu.VMEM)
        fields_out, image = pl.pallas_call(
            functools.partial(kernel, sizes),
            out_shape=(
                pltpu.VMEM(fields_in.shape, F32),
                pltpu.VMEM((per_lane, points), F32),
            ),
            in_specs=[anywhere] * 8,
            out_specs=(vmem, vmem),
            scratch_shapes=[
                pltpu.SMEM(codes.shape, jnp.int32),
                pltpu.VMEM(codes.shape, jnp.int32),
                pltpu.SMEM(slowness_table.shape, F32),
                pltpu.VMEM(shot_data.shape, F32),
                pltpu.VMEM(vel_index.shape, jnp.int32),
                pltpu.VMEM(fields_in.shape, F32),
                pltpu.VMEM(high.shape, BF16),
                pltpu.VMEM(low.shape, BF16),
                pltpu.VMEM(twist.shape, F32),
                pltpu.SemaphoreType.DMA((9,)),
                pltpu.VMEM((steps, 2, outer, rows, LANES), F32),
                pltpu.VMEM((steps, 2, outer, rows, LANES), F32),
                pltpu.VMEM((ticks, 2, outer, rows, LANES), F32),
                pltpu.VMEM((ticks, 2, outer, rows, LANES), F32),
                pltpu.VMEM((ticks, 2, outer // 2, rows, LANES), F32),
                pltpu.VMEM((ticks, depth_n - 1, 2, outer // 2, rows, LANES), F32),
                pltpu.VMEM((steps, outer, rows, LANES), F32),
                pltpu.VMEM((steps, outer, LANES), F32),
                pltpu.VMEM((per_lane, lane_n, outer, LANES), F32),
                pltpu.SemaphoreType.DMA((ticks,)),
                pltpu.SemaphoreType.DMA((ticks,)),
                pltpu.SemaphoreType.DMA((ticks,)),
                pltpu.SemaphoreType.DMA((ticks,)),
                pltpu.SemaphoreType.DMA((steps,)),
                pltpu.SemaphoreType.DMA((per_lane, lane_n)),
            ],
            compiler_params=pltpu.CompilerParams(collective_id=0, has_side_effects=True),
            name="migrate",
        )(
            codes, slowness_table, shot_data, vel_index, fields_in,
            jnp.asarray(high), jnp.asarray(low), jnp.asarray(twist),
        )
        return fields_out, image

    return jax.shard_map(
        per_device,
        mesh=mesh,
        in_specs=(
            P("depth", None, "lane", None),
            P(None, "depth", None, "lane", None),
            P(None, None, "lane"),
            P("depth", None),
            P(),
        ),
        out_specs=(P("depth", None, "lane", None), P(("depth", "lane"), None)),
        check_vma=False,
    )
```
